128 devices in a mesh: vae: 8 (over x_hi, z), seq: 16 (over x_lo, y, core).
Axes of the slice: x: 4 (x_hi: 2, x_lo: 2; x = x_hi * 2 + x_lo), y: 4, z: 4, core: 2. Of those that a mesh axis runs over, the one named last changes fastest.
Arguments:
- video: float32 [32, 256, 512], P('vae', 'seq')
- frame_counts: int32 [8], replicated, may hold values from 2 to 4, as said below
- conv_weight: float32 [3, 512, 512], replicated, may hold values from -0.15625 to 0.15625
- conv_bias: float32 [512], replicated, may hold values from -4 to 4
- norm_gain: float32 [512], replicated, may hold values from 0.1 to 1.9
- norm_bias: float32 [512], replicated, may hold values from -3 to 3
- embed_weight: bfloat16 [512, 3072], replicated, may hold values from -0.25 to 0.25
- embed_bias: float32 [3072], replicated, may hold values from -3 to 3
- shift: float32 [3072], replicated, may hold values from -3 to 3
- scale: float32 [3072], replicated, may hold values from -3 to 3
- gate: float32 [3072], replicated, may hold values from 1 to 3
- qkv_weight: bfloat16 [3072, 3, 3072], P(None, None, 'vae')
- q_gain: float32 [128], replicated, may hold values from 1 to 6
- k_gain: float32 [128], replicated, may hold values from 1 to 6
- out_weight: bfloat16 [3072, 3072], P('vae'), may hold values from -0.109375 to 0.109375
Outputs:
- result: bfloat16 [32, 256, 3072], P(None, 'seq', 'vae')
The draws below stay inside these ranges and needn't reach their ends.
Inputs may be any that keep to these rules, and one draw needn't show every extreme that they name: `frame_counts`: every index of vae has at least 2 live slots; at least one has all 4 live.
All inputs are finite; a program needn't handle non-finite values.
Results may differ from the reference program's by a relative error of at most 0.013.
The reference program's roundings to bfloat16 on the way count: a program that leaves them out, or rounds other values in their place, can miss the bound.
Values may be sent and summed in bfloat16 or wider, within the bound.
A program may use at most 192 MiB of HBM per device.

```python
import math
import jax
import jax.numpy as jnp
from jax import lax

C = 512
GROUPS = 32
D = 3072
HD = 128
F_DEV = 4
FRAMES = 32
POS = 256
HEADS = 24
N_VAE = 8


def draw_video(key, part):
    channel = jnp.exp(jax.random.uniform(jax.random.fold_in(key, 7), (C,), jnp.float32, 0.0, math.log(10.0)))
    signs = jnp.where(jax.random.uniform(jax.random.fold_in(key, 8), (C,), jnp.float32) < 0.5, -1.0, 1.0)
    frame_jitter = jnp.exp(jax.random.uniform(jax.random.fold_in(key, 9), (FRAMES,), jnp.float32, math.log(0.6), math.log(1.6)))
    place_jitter = jnp.exp(jax.random.uniform(jax.random.fold_in(key, 10), (POS,), jnp.float32, math.log(0.6), math.log(1.6)))
    frame_rise = (1.0 + 2.0 * jnp.arange(FRAMES, dtype=jnp.float32) / (FRAMES - 1)) * frame_jitter
    place_rise = (1.0 + 2.0 * jnp.arange(POS, dtype=jnp.float32) / (POS - 1)) * place_jitter
    common = 1.5 * jax.random.normal(jax.random.fold_in(key, 11), (FRAMES, POS), jnp.float32)
    base = jax.random.normal(key, (FRAMES, POS, C), jnp.float32)
    field = base + common[:, :, None] * signs[None, None, :]
    return field * frame_rise[:, None, None] * place_rise[None, :, None] * channel[None, None, :] * 0.3


def draw_frame_counts(key, part):
    counts = jax.random.randint(key, (N_VAE,), 2, F_DEV + 1)
    chosen = jax.random.randint(jax.random.fold_in(key, 3), (), 0, N_VAE)
    return jnp.where(jnp.arange(N_VAE) == chosen, F_DEV, counts).astype(jnp.int32)


def bounded_matrix(key):
    bound = 6.0 / math.sqrt(D)
    drawn = jax.random.normal(key, (D, HEADS * HD), jnp.float32) / math.sqrt(D)
    return jnp.clip(drawn, -bound, bound)


def draw_qkv_weight(key, part):
    query_part = bounded_matrix(jax.random.fold_in(key, 21))
    key_fresh = bounded_matrix(jax.random.fold_in(key, 22))
    value_part = bounded_matrix(jax.random.fold_in(key, 23))
    key_part = key_fresh
    return jnp.stack([query_part, key_part, value_part], axis=1).astype(jnp.bfloat16)


def gain_values(key):
    return jnp.exp(jax.random.uniform(key, (HD,), jnp.float32, 0.0, math.log(2.0)))


def draw_q_gain(key, part):
    return gain_values(jax.random.fold_in(key, 41))


def draw_k_gain(key, part):
    return gain_values(jax.random.fold_in(key, 42))


def level_of(own_key, dims, pieces, low, top_value):
    def one(dim, shards_of):
        draws = jax.random.uniform(jax.random.fold_in(jax.random.fold_in(own_key, 6), dim), (shards_of,), jnp.float32, low / len(pieces), top_value / len(pieces))
        return jnp.repeat(jnp.exp(draws), dims[dim] // shards_of).reshape((-1,) + (1,) * (len(dims) - dim - 1))

    gain = one(*pieces[0])
    for cut in pieces[1:]:
        gain = gain * one(*cut)
    return gain


def scatter_about(rng, shape, deviation, reach, split=(), kind=jnp.bfloat16):
    values = jax.random.normal(rng, shape, jnp.float32) * deviation
    if len(split) > 0:
        values = level_of(rng, shape, split, -0.22, 0.18) * values
    return jnp.clip(values, min=-reach, max=reach).astype(kind)


def setup_inputs(seed: int = 0) -> dict:
    streams_of = jax.random.split(jax.random.key(seed), 16)
    video = draw_video(jax.random.fold_in(streams_of[15], 71), 0)
    frame_counts = draw_frame_counts(jax.random.fold_in(streams_of[15], 71), 0)
    conv_weight = scatter_about(streams_of[2], (3, C, C), (3 * C) ** -0.5, 0.15625, (), jnp.float32)
    conv_bias = scatter_about(streams_of[3], (C,), 1.0, 4.0, (), jnp.float32)
    norm_gain = jnp.clip(1.0 + 0.18 * jax.random.normal(streams_of[4], (C,), jnp.float32), 0.1, 1.9)
    norm_bias = scatter_about(streams_of[5], (C,), 0.5, 3.0, (), jnp.float32)
    embed_weight = scatter_about(streams_of[6], (C, D), C ** -0.5, 0.25)
    embed_bias = scatter_about(streams_of[7], (D,), 0.5, 3.0, (), jnp.float32)
    shift = scatter_about(streams_of[8], (D,), 0.5, 3.0, (), jnp.float32)
    scale = scatter_about(streams_of[9], (D,), 0.5, 3.0, (), jnp.float32)
    gate = jnp.clip(jax.random.uniform(streams_of[10], (D,), jnp.float32, 1.0, 3.0), 1.0, 3.0)
    qkv_weight = draw_qkv_weight(jax.random.fold_in(streams_of[15], 71), 0)
    q_gain = draw_q_gain(jax.random.fold_in(streams_of[15], 71), 0)
    k_gain = draw_k_gain(jax.random.fold_in(streams_of[15], 71), 0)
    out_weight = scatter_about(streams_of[14], (HEADS * HD, D), (HEADS * HD) ** -0.5, 0.109375, ((0, 8),))
    return dict(video=video, frame_counts=frame_counts, conv_weight=conv_weight, conv_bias=conv_bias, norm_gain=norm_gain, norm_bias=norm_bias, embed_weight=embed_weight, embed_bias=embed_bias, shift=shift, scale=scale, gate=gate, qkv_weight=qkv_weight, q_gain=q_gain, k_gain=k_gain, out_weight=out_weight)


def head_norm(values, weights):
    return values * lax.rsqrt(lax.optimization_barrier(jnp.mean(values * values, axis=-1, keepdims=True)) + 1e-06) * weights

def reference(video, frame_counts, conv_weight, conv_bias, norm_gain, norm_bias, embed_weight, embed_bias, shift, scale, gate, qkv_weight, q_gain, k_gain, out_weight):
    highest = lax.Precision.HIGHEST
    slots = jnp.arange(FRAMES, dtype=jnp.int32)
    shard = slots // F_DEV
    within = slots % F_DEV
    counts = frame_counts.astype(jnp.int32)
    offsets = (jnp.cumsum(counts) - counts).astype(jnp.int32)
    valid = within < counts[shard]
    times = (offsets[shard] + within).astype(jnp.int32)
    target = jnp.where(valid, times, FRAMES).astype(jnp.int32)
    clip = jnp.zeros((FRAMES + 1, POS, C), jnp.float32).at[target].set(video)[:FRAMES]
    padded = jnp.concatenate([jnp.zeros((2, POS, C), jnp.float32), clip], 0)
    conv = conv_bias + jnp.zeros((FRAMES, POS, C), jnp.float32)
    for tap in range(3):
        conv = conv + jnp.einsum('fpc,cd->fpd', padded[2 - tap:2 - tap + FRAMES], conv_weight[tap], precision=highest)
    after = conv[jnp.minimum(times, FRAMES - 1)]
    live = valid.astype(jnp.float32)[:, None, None]
    masked = after * live
    width = C // GROUPS
    first = masked.reshape(FRAMES, POS, GROUPS, width).sum((0, 1, 3))
    second = (masked * after).reshape(FRAMES, POS, GROUPS, width).sum((0, 1, 3))
    number = jnp.sum(counts).astype(jnp.float32) * (POS * width)
    mean = first / number
    var = second / number - mean * mean
    centre = jnp.repeat(mean, width)
    inverse = jnp.repeat(lax.rsqrt(var + 1e-06), width)
    act = jax.nn.silu((after - centre) * inverse * norm_gain + norm_bias).astype(jnp.bfloat16)
    row_live = jnp.repeat(valid.astype(jnp.float32), POS)[:, None]
    tokens = ((jnp.dot(act.reshape(-1, C), embed_weight, preferred_element_type=jnp.float32) + embed_bias) * row_live).astype(jnp.bfloat16)
    rows = tokens.astype(jnp.float32)
    centred = rows - lax.optimization_barrier(jnp.mean(rows, axis=-1, keepdims=True))
    spread = lax.optimization_barrier(jnp.mean(centred * centred, axis=-1, keepdims=True))
    hidden = (centred * lax.rsqrt(spread + 1e-06) * (1.0 + scale) + shift).astype(jnp.bfloat16)
    inner = HEADS * HD
    proj = jnp.dot(hidden, qkv_weight.reshape(D, 3 * inner), preferred_element_type=jnp.float32)
    total = rows.shape[0]
    queries = head_norm(proj[:, :inner].reshape(total, HEADS, HD), q_gain).astype(jnp.bfloat16)
    keys = head_norm(proj[:, inner:2 * inner].reshape(total, HEADS, HD), k_gain).astype(jnp.bfloat16)
    values = proj[:, 2 * inner:].reshape(total, HEADS, HD).astype(jnp.bfloat16)
    key_live = row_live[:, 0] > 0.5

    def one_head(index):
        query = lax.dynamic_index_in_dim(queries, index, 1, keepdims=False)
        key = lax.dynamic_index_in_dim(keys, index, 1, keepdims=False)
        value = lax.dynamic_index_in_dim(values, index, 1, keepdims=False)
        scores = jnp.dot(query, key.T, preferred_element_type=jnp.float32) / math.sqrt(HD)
        scores = jnp.where(key_live[None, :], scores, -1e+30)
        top = lax.optimization_barrier(jnp.max(scores, axis=-1, keepdims=True))
        weights = jnp.where(key_live[None, :], jnp.exp(scores - top), 0.0)
        summed = lax.optimization_barrier(jnp.sum(weights, axis=-1))
        return jnp.dot(weights.astype(jnp.bfloat16), value, preferred_element_type=jnp.float32) / summed[:, None]
    heads_out = lax.map(one_head, jnp.arange(HEADS, dtype=jnp.int32))
    merged = jnp.transpose(heads_out, (1, 0, 2)).reshape(total, inner).astype(jnp.bfloat16)
    attn = jnp.dot(merged, out_weight, preferred_element_type=jnp.float32)
    result = ((rows + gate * attn) * row_live).astype(jnp.bfloat16)
    return result.reshape(FRAMES, POS, D)
```

```python
import functools
import math

import jax
import jax.numpy as jnp
from jax import lax
from jax.experimental import pallas as pl
from jax.experimental.pallas import tpu as pltpu
from jax.sharding import PartitionSpec as P

GROUPS = 32
HD = 128
NV = 8
NS = 16
F32 = jnp.float32
BF16 = jnp.bfloat16
MESH = pl.DeviceIdType.MESH


def mod(a, n):
    return lax.rem(a + n, n)


def tokens_kernel(
    video, counts, conv_w, conv_b, norm_g, norm_b, embed_w, embed_b, shift, scale,
    hidden, resid,
    halo, w_hi, w_lo, sums_v, sums_s, act, tokens,
    halo_sem, ssem1, rsem1, ssem2, rsem2, asend, arecv,
):
    v = lax.axis_index("vae")
    s = lax.axis_index("seq")
    rows, chans = video.shape
    pdev = 16
    width = chans // GROUPS

    barrier = pltpu.get_barrier_semaphore()
    for d in range(1, NV):
        pl.semaphore_signal(barrier, inc=1, device_id=(mod(v + d, NV), s), device_id_type=MESH)
    for d in range(1, NS):
        pl.semaphore_signal(barrier, inc=1, device_id=(v, mod(s + d, NS)), device_id_type=MESH)

    @pl.when(v == 0)
    def _():
        halo[...] = jnp.zeros_like(halo)

    pl.semaphore_wait(barrier, NV - 1 + NS - 1)
    halo_copy = pltpu.make_async_remote_copy(
        src_ref=video, dst_ref=halo, send_sem=halo_sem.at[0], recv_sem=halo_sem.at[1],
        device_id=(mod(v + 1, NV), s), device_id_type=MESH,
    )

    @pl.when(v < NV - 1)
    def _():
        halo_copy.start()

    for tap in range(3):
        w = conv_w[tap]
        hi = w.astype(BF16)
        w_hi[tap] = hi
        w_lo[tap] = (w - hi.astype(F32)).astype(BF16)

    mine = counts[v]
    before = counts[jnp.maximum(v - 1, 0)]

    @pl.when(v > 0)
    def _():
        halo_copy.wait_recv()

    prior = jnp.where(
        before == 2, halo[0:32], jnp.where(before == 3, halo[16:48], halo[32:64])
    )
    ext = jnp.concatenate([prior, video[...]], 0)
    e_hi = ext.astype(BF16)
    e_lo = (ext - e_hi.astype(F32)).astype(BF16)
    both = jnp.zeros((2 * rows, chans), F32)
    low = jnp.zeros((rows, chans), F32)
    for tap in range(3):
        a = 32 - 16 * tap
        x_hi = e_hi[a : a + rows]
        both += jnp.dot(
            jnp.concatenate([x_hi, e_lo[a : a + rows]], 0), w_hi[tap], preferred_element_type=F32
        )
        low += jnp.dot(x_hi, w_lo[tap], preferred_element_type=F32)
    conv = both[:rows] + (both[rows:] + low) + conv_b[...]
    row_frame = lax.broadcasted_iota(jnp.int32, (rows, chans), 0) // pdev
    masked = jnp.where(row_frame < mine, conv, 0.0)
    first = jnp.sum(masked, axis=0, keepdims=True)
    second = jnp.sum(masked * conv, axis=0, keepdims=True)
    sums_v[v] = jnp.concatenate([first, second], 0)

    @pl.when(v < NV - 1)
    def _():
        halo_copy.wait_send()

    sends = []
    for d in range(1, NV):
        c = pltpu.make_async_remote_copy(
            src_ref=sums_v.at[v], dst_ref=sums_v.at[v], send_sem=ssem1.at[d], recv_sem=rsem1.at[d],
            device_id=(mod(v + d, NV), s), device_id_type=MESH,
        )
        c.start()
        sends.append(c)
    for c in sends:
        c.wait()
    total = sums_v[0]
    for u in range(1, NV):
        total += sums_v[u]
    sums_s[s] = total
    sends = []
    for d in range(1, NS):
        c = pltpu.make_async_remote_copy(
            src_ref=sums_s.at[s], dst_ref=sums_s.at[s], send_sem=ssem2.at[d], recv_sem=rsem2.at[d],
            device_id=(v, mod(s + d, NS)), device_id_type=MESH,
        )
        c.start()
        sends.append(c)
    gi = lax.broadcasted_iota(jnp.int32, (chans, chans), 0) // width
    gj = lax.broadcasted_iota(jnp.int32, (chans, chans), 1) // width
    same = jnp.where(gi == gj, 1.0, 0.0).astype(BF16)
    live = counts[0]
    for u in range(1, NV):
        live += counts[u]
    for c in sends:
        c.wait()
    total = sums_s[0]
    for u in range(1, NS):
        total += sums_s[u]
    p1 = total.astype(BF16)
    r1 = total - p1.astype(F32)
    p2 = r1.astype(BF16)
    p3 = (r1 - p2.astype(F32)).astype(BF16)
    grouped = (
        jnp.dot(p3, same, preferred_element_type=F32)
        + jnp.dot(p2, same, preferred_element_type=F32)
        + jnp.dot(p1, same, preferred_element_type=F32)
    )
    number = live.astype(F32) * (pdev * NS * width)
    mean = grouped[0:1] / number
    var = grouped[1:2] / number - mean * mean
    y = (conv - mean) * lax.rsqrt(var + 1e-06) * norm_g[...] + norm_b[...]
    act[v] = (y / (1.0 + jnp.exp(-y))).astype(BF16)

    far = mod(v + 4, NV)
    base = (v // 4) * 4
    fbase = 4 - base
    z = lax.rem(v, 4)
    up, down, opp = mod(z + 1, 4), mod(z - 1, 4), mod(z + 2, 4)
    half = rows // 2

    def hop(slot, lo, n, dev, sem_s, sem_r):
        ref = act.at[slot, pl.ds(lo, n)]
        return pltpu.make_async_remote_copy(
            src_ref=ref, dst_ref=ref, send_sem=asend.at[sem_s], recv_sem=arecv.at[sem_r],
            device_id=(dev, s), device_id_type=MESH,
        )

    far_c = hop(v, 0, rows, far, 0, 0)
    up_c = hop(v, 0, rows, base + up, 1, 1)
    dn_c = hop(v, 0, rows, base + down, 2, 2)
    far_c.start()
    up_c.start()
    dn_c.start()
    far_c.wait_recv()
    fup_c = hop(far, 0, rows, base + up, 3, 3)
    fdn_c = hop(far, 0, rows, base + down, 4, 4)
    fup_c.start()
    fdn_c.start()
    up_c.wait_recv()
    o1 = hop(base + down, 0, half, base + up, 5, 5)
    o1.start()
    dn_c.wait_recv()
    o2 = hop(base + up, half, half, base + down, 6, 6)
    o2.start()
    fup_c.wait_recv()
    o3 = hop(fbase + down, 0, half, base + up, 7, 7)
    o3.start()
    fdn_c.wait_recv()
    o4 = hop(fbase + up, half, half, base + down, 8, 8)
    o4.start()
    for c in (o1, o2, o3, o4):
        c.wait_recv()
    for c in (far_c, up_c, dn_c, fup_c, fdn_c, o1, o2, o3, o4):
        c.wait_send()

    total_rows = NV * rows
    dwidth = embed_w.shape[1]
    idx = lax.broadcasted_iota(jnp.int32, (total_rows, 1), 0)
    limit = jnp.zeros((total_rows, 1), jnp.int32)
    for u in range(NV):
        limit = jnp.where(idx // rows == u, counts[u], limit)
    alive = (lax.rem(idx, rows) // pdev < limit).astype(F32)
    a = act[...].reshape(total_rows, chans)
    tile = 512
    acc = jnp.zeros((total_rows, 128), F32)
    for t in range(dwidth // tile):
        sl = pl.ds(t * tile, tile)
        tok = jnp.dot(a, embed_w[:, sl], preferred_element_type=F32) + embed_b[:, sl]
        tok = (tok * alive).astype(BF16)
        tokens[:, sl] = tok
        tf = tok.astype(F32)
        for q in range(tile // 128):
            acc += tf[:, q * 128 : (q + 1) * 128]
    mu = jnp.sum(acc, axis=1, keepdims=True) * (1.0 / dwidth)
    acc = jnp.zeros((total_rows, 128), F32)
    for t in range(dwidth // tile):
        tf = tokens[:, pl.ds(t * tile, tile)].astype(F32) - mu
        for q in range(tile // 128):
            cut = tf[:, q * 128 : (q + 1) * 128]
            acc += cut * cut
    inv = lax.rsqrt(jnp.sum(acc, axis=1, keepdims=True) * (1.0 / dwidth) + 1e-06)
    for t in range(dwidth // tile):
        sl = pl.ds(t * tile, tile)
        tf = tokens[:, sl].astype(F32) - mu
        hidden[:, sl] = (tf * inv * (1.0 + scale[:, sl]) + shift[:, sl]).astype(BF16)
    cols = dwidth // NV
    resid[...] = tokens[:, pl.ds(pl.multiple_of(v * cols, 128), cols)]


def tokens_call(video, counts, conv_w, conv_b, norm_g, norm_b, embed_w, embed_b, shift, scale):
    rows, chans = video.shape
    dwidth = embed_w.shape[1]
    vm = pl.BlockSpec(memory_space=pltpu.VMEM)
    return pl.pallas_call(
        tokens_kernel,
        name="tokens",
        out_shape=(
            jax.ShapeDtypeStruct((NV * rows, dwidth), BF16),
            jax.ShapeDtypeStruct((NV * rows, dwidth // NV), BF16),
        ),
        in_specs=[vm, pl.BlockSpec(memory_space=pltpu.SMEM)] + [vm] * 8,
        out_specs=(vm, vm),
        scratch_shapes=[
            pltpu.VMEM((rows, chans), F32),
            pltpu.VMEM((3, chans, chans), BF16),
            pltpu.VMEM((3, chans, chans), BF16),
            pltpu.VMEM((NV, 2, chans), F32),
            pltpu.VMEM((NS, 2, chans), F32),
            pltpu.VMEM((NV, rows, chans), BF16),
            pltpu.VMEM((NV * rows, dwidth), BF16),
            pltpu.SemaphoreType.DMA((2,)),
            pltpu.SemaphoreType.DMA((NV,)),
            pltpu.SemaphoreType.DMA((NV,)),
            pltpu.SemaphoreType.DMA((NS,)),
            pltpu.SemaphoreType.DMA((NS,)),
            pltpu.SemaphoreType.DMA((9,)),
            pltpu.SemaphoreType.DMA((9,)),
        ],
        compiler_params=pltpu.CompilerParams(
            collective_id=0, has_side_effects=True, vmem_limit_bytes=40 * 2**20
        ),
    )(video, counts, conv_w, conv_b, norm_g, norm_b, embed_w, embed_b, shift, scale)

def flash_kernel(live, q_ref, k_ref, vt_ref, o_ref):
    nloc = q_ref.shape[1]
    q = q_ref[0]
    pdev = 16
    nseq = k_ref.shape[1]
    idx = lax.broadcasted_iota(jnp.int32, (nloc, 1), 0) // (4 * pdev)
    limit = jnp.zeros((nloc, 1), jnp.int32)
    for u in range(NV):
        limit = jnp.where(idx == u, live[u], limit)
    frame = lax.rem(lax.broadcasted_iota(jnp.int32, (nloc, 1), 0), 4 * pdev) // pdev
    bias = jnp.where(frame < limit, 0.0, -1e30)
    coef = math.log2(math.e) / math.sqrt(HD)

    def step(j, carry):
        m, l, acc = carry
        st = lax.dot_general(k_ref[0, j], q, (((1,), (1,)), ((), ())), preferred_element_type=F32)
        st = st * coef + bias
        new = jnp.maximum(m, jnp.max(st, axis=0, keepdims=True))
        alpha = jnp.exp2(m - new)
        p = jnp.exp2(st - new)
        l = l * alpha + jnp.sum(p, axis=0, keepdims=True)
        acc = acc * alpha + jnp.dot(vt_ref[0, j], p.astype(BF16), preferred_element_type=F32)
        return new, l, acc

    m0 = jnp.full((1, nloc), -1e30, F32)
    m, l, acc = lax.fori_loop(
        0, nseq, step, (m0, jnp.zeros((1, nloc), F32), jnp.zeros((HD, nloc), F32))
    )
    o_ref[...] = jnp.transpose(acc / l).astype(BF16)


def flash_call(live, q, k, vt):
    heads, nloc, _ = q.shape
    nseq = k.shape[1]
    return pl.pallas_call(
        flash_kernel,
        name="flash",
        grid=(heads,),
        out_shape=jax.ShapeDtypeStruct((nloc, heads * HD), BF16),
        in_specs=[
            pl.BlockSpec(memory_space=pltpu.SMEM),
            pl.BlockSpec((1, nloc, HD), lambda h: (h, 0, 0)),
            pl.BlockSpec((1, nseq, nloc, HD), lambda h: (h, 0, 0, 0)),
            pl.BlockSpec((1, nseq, HD, nloc), lambda h: (h, 0, 0, 0)),
        ],
        out_specs=pl.BlockSpec((nloc, HD), lambda h: (0, h)),
        compiler_params=pltpu.CompilerParams(vmem_limit_bytes=40 * 2**20),
    )(live, q, k, vt)


def head_norm(values, weights):
    return values * lax.rsqrt(jnp.mean(values * values, axis=-1, keepdims=True) + 1e-06) * weights


def body(
    video, frame_counts, conv_weight, conv_bias, norm_gain, norm_bias, embed_weight, embed_bias,
    shift, scale, gate, qkv_weight, q_gain, k_gain, out_weight,
):
    fdev, pdev, chans = video.shape
    me_vae = lax.axis_index("vae")
    row = lambda a: a.reshape(1, -1)
    hidden, resid = tokens_call(
        video.reshape(fdev * pdev, chans), frame_counts, conv_weight, row(conv_bias),
        row(norm_gain), row(norm_bias), embed_weight, row(embed_bias), row(shift), row(scale),
    )
    nloc, dwidth = hidden.shape
    cols = dwidth // NV
    w_cols = lax.all_to_all(
        out_weight.reshape(cols, NV, cols), "vae", split_axis=1, concat_axis=0, tiled=False
    ).reshape(dwidth, cols)
    w3 = jnp.transpose(qkv_weight, (1, 0, 2))
    heads = w3.shape[2] // HD
    proj = [jnp.dot(hidden, w3[i], preferred_element_type=F32) for i in range(3)]
    queries = head_norm(proj[0].reshape(nloc, heads, HD), q_gain).astype(BF16)
    keys = head_norm(proj[1].reshape(nloc, heads, HD), k_gain).astype(BF16)
    values = proj[2].reshape(nloc, heads, HD).astype(BF16)
    k_all = lax.all_gather(jnp.transpose(keys, (1, 0, 2)), "seq", axis=1)
    v_all = lax.all_gather(jnp.transpose(values, (1, 2, 0)), "seq", axis=1)
    o = flash_call(frame_counts, jnp.transpose(queries, (1, 0, 2)), k_all, v_all)
    o_all = lax.all_gather(o, "vae", axis=0)
    merged = jnp.transpose(o_all, (1, 0, 2)).reshape(nloc, dwidth)
    mixed = jnp.dot(merged, w_cols, preferred_element_type=F32)
    gate_part = lax.dynamic_slice_in_dim(gate, me_vae * cols, cols, 0)
    alive = (jnp.arange(fdev)[None, :] < frame_counts[:, None]).astype(F32)
    alive = jnp.broadcast_to(alive[:, :, None], (NV, fdev, pdev)).reshape(nloc, 1)
    result = ((resid.astype(F32) + gate_part * mixed) * alive).astype(BF16)
    return result.reshape(fdev * NV, pdev, cols)


def solution(mesh):
    in_specs = (
        P("vae", "seq", None), P(), P(), P(), P(), P(), P(), P(), P(), P(), P(),
        P(None, None, "vae"), P(), P(), P("vae", None),
    )
    return jax.shard_map(
        body, mesh=mesh, in_specs=in_specs, out_specs=P(None, "seq", "vae"), check_vma=False
    )
```

```python
import functools
import math

import jax
import jax.numpy as jnp
from jax import lax
from jax.experimental import pallas as pl
from jax.experimental.pallas import tpu as pltpu
from jax.sharding import PartitionSpec as P

GROUPS = 32
HD = 128
NV = 8
NS = 16
F32 = jnp.float32
BF16 = jnp.bfloat16
MESH = pl.DeviceIdType.MESH


def mod(a, n):
    return lax.rem(a + n, n)


def fused_kernel(
    video, counts, conv_w_hbm, conv_b, norm_g, norm_b, embed_w_hbm, embed_b, shift, scale,
    gate, w3_hbm, q_gain, k_gain, out_w,
    result,
    conv_w, embed_w, w3,
    halo, w_hi, w_lo, sums_v, sums_s, act, tokens, hidden,
    kbuf, vbuf, qbuf, obuf, wcols,
    load_sem, halo_sem, ssem1, rsem1, ssem2, rsem2, asend, arecv,
    wsend, wrecv, ksend, krecv, vrecv, osend, orecv,
):
    v = lax.axis_index("vae")
    s = lax.axis_index("seq")
    rows, chans = video.shape
    pdev = 16
    width = chans // GROUPS
    dwidth = embed_b.shape[1]
    cols = dwidth // NV
    heads = cols // HD
    nloc = NV * rows

    loads = [
        pltpu.make_async_copy(conv_w_hbm, conv_w, load_sem.at[0]),
        pltpu.make_async_copy(embed_w_hbm, embed_w, load_sem.at[1]),
        pltpu.make_async_copy(w3_hbm, w3, load_sem.at[2]),
    ]
    for c in loads:
        c.start()

    xl = s // 8
    y = lax.rem(s, 8) // 2
    core = lax.rem(s, 2)
    r = lax.rem(s, 8)

    def place(dx, dy, dc):
        return mod(xl + dx, 2) * 8 + mod(y + dy, 4) * 2 + mod(core + dc, 2)

    part_rows = cols // 8
    own_w = pltpu.make_async_copy(
        out_w.at[pl.ds(r * part_rows, part_rows), pl.ds(pl.multiple_of(v * cols, 128), cols)],
        wcols.at[v, pl.ds(r * part_rows, part_rows)],
        load_sem.at[3],
    )
    own_w.start()

    barrier = pltpu.get_barrier_semaphore()
    for d in range(1, NV):
        pl.semaphore_signal(barrier, inc=1, device_id=(mod(v + d, NV), s), device_id_type=MESH)
    for d in range(1, NS):
        pl.semaphore_signal(barrier, inc=1, device_id=(v, mod(s + d, NS)), device_id_type=MESH)

    @pl.when(v == 0)
    def _():
        halo[...] = jnp.zeros_like(halo)

    pl.semaphore_wait(barrier, NV - 1 + NS - 1)
    halo_copy = pltpu.make_async_remote_copy(
        src_ref=video, dst_ref=halo, send_sem=halo_sem.at[0], recv_sem=halo_sem.at[1],
        device_id=(mod(v + 1, NV), s), device_id_type=MESH,
    )

    @pl.when(v < NV - 1)
    def _():
        halo_copy.start()

    w_first = []
    for d in range(1, NV):
        u = mod(v + d, NV)
        c = pltpu.make_async_remote_copy(
            src_ref=out_w.at[
                pl.ds(r * part_rows, part_rows), pl.ds(pl.multiple_of(u * cols, 128), cols)
            ],
            dst_ref=wcols.at[v, pl.ds(r * part_rows, part_rows)],
            send_sem=wsend.at[d], recv_sem=wrecv.at[d],
            device_id=(u, s), device_id_type=MESH,
        )
        c.start()
        w_first.append(c)

    loads[0].wait()
    for tap in range(3):
        w = conv_w[tap]
        hi = w.astype(BF16)
        w_hi[tap] = hi
        w_lo[tap] = (w - hi.astype(F32)).astype(BF16)

    mine = counts[v]
    before = counts[jnp.maximum(v - 1, 0)]

    @pl.when(v > 0)
    def _():
        halo_copy.wait_recv()

    prior = jnp.where(
        before == 2, halo[0:32], jnp.where(before == 3, halo[16:48], halo[32:64])
    )
    ext = jnp.concatenate([prior, video[...]], 0)
    e_hi = ext.astype(BF16)
    e_lo = (ext - e_hi.astype(F32)).astype(BF16)
    both = jnp.zeros((2 * rows, chans), F32)
    low = jnp.zeros((rows, chans), F32)
    for tap in range(3):
        a = 32 - 16 * tap
        x_hi = e_hi[a : a + rows]
        both += jnp.dot(
            jnp.concatenate([x_hi, e_lo[a : a + rows]], 0), w_hi[tap], preferred_element_type=F32
        )
        low += jnp.dot(x_hi, w_lo[tap], preferred_element_type=F32)
    conv = both[:rows] + (both[rows:] + low) + conv_b[...]
    row_frame = lax.broadcasted_iota(jnp.int32, (rows, chans), 0) // pdev
    masked = jnp.where(row_frame < mine, conv, 0.0)
    first = jnp.sum(masked, axis=0, keepdims=True)
    second = jnp.sum(masked * conv, axis=0, keepdims=True)
    sums_v[v] = jnp.concatenate([first, second], 0)

    @pl.when(v < NV - 1)
    def _():
        halo_copy.wait_send()

    sends = []
    for d in range(1, NV):
        c = pltpu.make_async_remote_copy(
            src_ref=sums_v.at[v], dst_ref=sums_v.at[v], send_sem=ssem1.at[d], recv_sem=rsem1.at[d],
            device_id=(mod(v + d, NV), s), device_id_type=MESH,
        )
        c.start()
        sends.append(c)
    gi = lax.broadcasted_iota(jnp.int32, (chans, chans), 0) // width
    gj = lax.broadcasted_iota(jnp.int32, (chans, chans), 1) // width
    same = jnp.where(gi == gj, 1.0, 0.0).astype(BF16)
    live = counts[0]
    for u in range(1, NV):
        live += counts[u]
    own_w.wait()
    for c in w_first:
        c.wait()
    for c in sends:
        c.wait()
    total = sums_v[0]
    for u in range(1, NV):
        total += sums_v[u]
    sums_s[s] = total
    sends = []
    for d in range(1, NS):
        c = pltpu.make_async_remote_copy(
            src_ref=sums_s.at[s], dst_ref=sums_s.at[s], send_sem=ssem2.at[d], recv_sem=rsem2.at[d],
            device_id=(v, mod(s + d, NS)), device_id_type=MESH,
        )
        c.start()
        sends.append(c)

    def w_hop(dy, lo, n, dev, sem):
        rr = mod(y + dy, 4) * 2 + core
        ref = wcols.at[pl.ds(lo, n), pl.ds(rr * part_rows, part_rows)]
        return pltpu.make_async_remote_copy(
            src_ref=ref, dst_ref=ref, send_sem=wsend.at[sem], recv_sem=wrecv.at[sem],
            device_id=(v, dev), device_id_type=MESH,
        )

    partner = place(0, 0, 1)
    y_up, y_dn = place(0, 1, 0), place(0, 3, 0)
    w_up = w_hop(0, 0, NV, y_up, 8)
    w_dn = w_hop(0, 0, NV, y_dn, 9)
    w_pt = w_hop(0, 0, NV, partner, 10)

    for c in sends:
        c.wait()
    w_up.start()
    w_dn.start()
    w_pt.start()
    total = sums_s[0]
    for u in range(1, NS):
        total += sums_s[u]
    p1 = total.astype(BF16)
    r1 = total - p1.astype(F32)
    p2 = r1.astype(BF16)
    p3 = (r1 - p2.astype(F32)).astype(BF16)
    grouped = (
        jnp.dot(p3, same, preferred_element_type=F32)
        + jnp.dot(p2, same, preferred_element_type=F32)
        + jnp.dot(p1, same, preferred_element_type=F32)
    )
    number = live.astype(F32) * (pdev * NS * width)
    mean = grouped[0:1] / number
    var = grouped[1:2] / number - mean * mean
    yv = (conv - mean) * lax.rsqrt(var + 1e-06) * norm_g[...] + norm_b[...]
    act[v] = (yv / (1.0 + jnp.exp(-yv))).astype(BF16)

    far = mod(v + 4, NV)
    base = (v // 4) * 4
    fbase = 4 - base
    z = lax.rem(v, 4)
    up, down = mod(z + 1, 4), mod(z - 1, 4)

    def vae_gather(view, n, send, recv):
        half = n // 2

        def hop(slot, lo, cnt, dev, sem):
            ref = view(slot, lo, cnt)
            return pltpu.make_async_remote_copy(
                src_ref=ref, dst_ref=ref, send_sem=send(sem), recv_sem=recv(sem),
                device_id=(dev, s), device_id_type=MESH,
            )

        far_c = hop(v, 0, n, far, 0)
        up_c = hop(v, 0, n, base + up, 1)
        dn_c = hop(v, 0, n, base + down, 2)
        fup_c = hop(far, 0, n, base + up, 3)
        fdn_c = hop(far, 0, n, base + down, 4)
        o1 = hop(base + down, 0, half, base + up, 5)
        o2 = hop(base + up, half, half, base + down, 6)
        o3 = hop(fbase + down, 0, half, base + up, 7)
        o4 = hop(fbase + up, half, half, base + down, 8)

        def one():
            far_c.start()
            up_c.start()
            dn_c.start()

        def two():
            far_c.wait_recv()
            fup_c.start()
            fdn_c.start()
            up_c.wait_recv()
            o1.start()
            dn_c.wait_recv()
            o2.start()

        def three():
            fup_c.wait_recv()
            o3.start()
            fdn_c.wait_recv()
            o4.start()

        def four():
            for c in (o1, o2, o3, o4):
                c.wait_recv()

        def five():
            for c in (far_c, up_c, dn_c, fup_c, fdn_c, o1, o2, o3, o4):
                c.wait_send()

        return one, two, three, four, five

    g = vae_gather(
        lambda slot, lo, n: act.at[slot, pl.ds(lo, n)],
        rows,
        lambda i: asend.at[i],
        lambda i: arecv.at[i],
    )
    g[0]()
    g[1]()
    w_up.wait_recv()
    w_r1 = w_hop(3, 0, NV // 2, y_up, 11)
    w_p1 = w_hop(3, 0, NV, partner, 12)
    w_r1.start()
    w_p1.start()
    w_dn.wait_recv()
    w_r2 = w_hop(1, NV // 2, NV // 2, y_dn, 13)
    w_p2 = w_hop(1, 0, NV, partner, 14)
    w_r2.start()
    w_p2.start()
    g[2]()
    g[3]()
    g[4]()

    idx = lax.broadcasted_iota(jnp.int32, (nloc, 1), 0)
    limit = jnp.zeros((nloc, 1), jnp.int32)
    for u in range(NV):
        limit = jnp.where(idx // rows == u, counts[u], limit)
    alive = (lax.rem(idx, rows) // pdev < limit).astype(F32)
    loads[1].wait()
    a = act[...].reshape(nloc, chans)
    tile = 512
    acc = jnp.zeros((nloc, 128), F32)
    for t in range(dwidth // tile):
        sl = pl.ds(t * tile, tile)
        tok = jnp.dot(a, embed_w[:, sl], preferred_element_type=F32) + embed_b[:, sl]
        tok = (tok * alive).astype(BF16)
        tokens[:, sl] = tok
        tf = tok.astype(F32)
        for q in range(tile // 128):
            acc += tf[:, q * 128 : (q + 1) * 128]
    mu = jnp.sum(acc, axis=1, keepdims=True) * (1.0 / dwidth)
    acc = jnp.zeros((nloc, 128), F32)
    for t in range(dwidth // tile):
        tf = tokens[:, pl.ds(t * tile, tile)].astype(F32) - mu
        for q in range(tile // 128):
            cut = tf[:, q * 128 : (q + 1) * 128]
            acc += cut * cut
    inv = lax.rsqrt(jnp.sum(acc, axis=1, keepdims=True) * (1.0 / dwidth) + 1e-06)
    for t in range(dwidth // tile):
        sl = pl.ds(t * tile, tile)
        tf = tokens[:, sl].astype(F32) - mu
        hidden[:, sl] = (tf * inv * (1.0 + scale[:, sl]) + shift[:, sl]).astype(BF16)

    x_to = place(1, 0, 0)

    def kv_hop(h, is_v, slot, part, dev, sem):
        buf, rec = (vbuf, vrecv) if is_v else (kbuf, krecv)
        n = HD if is_v else nloc
        if part is None:
            ref, ri = buf.at[h, slot], 0
        else:
            ref, ri = buf.at[h, slot, pl.ds(part * (n // 2), n // 2)], part
        return pltpu.make_async_remote_copy(
            src_ref=ref, dst_ref=ref, send_sem=ksend.at[h, sem], recv_sem=rec.at[h, slot, ri],
            device_id=(v, dev), device_id_type=MESH,
        )

    SENDS = {
        1: [
            (iv, (0, 0, 0), None, dev)
            for iv in (0, 1)
            for dev in ("x", "up", "dn", "pt")
        ],
        2: [
            (0, (1, 0, 0), None, "up"),
            (0, (1, 0, 0), None, "dn"),
            (0, (1, 0, 0), None, "pt"),
            (0, (0, 3, 0), 0, "up"),
            (0, (0, 3, 0), None, "pt"),
            (0, (0, 1, 0), 1, "dn"),
            (0, (0, 1, 0), None, "pt"),
            (1, (0, 3, 0), 0, "up"),
            (1, (0, 3, 0), None, "x"),
            (1, (0, 3, 0), None, "pt"),
            (1, (0, 1, 0), 1, "dn"),
            (1, (0, 1, 0), None, "x"),
            (1, (0, 1, 0), None, "pt"),
            (1, (1, 0, 0), None, "pt"),
        ],
        3: [
            (0, (1, 3, 0), 0, "up"),
            (0, (1, 3, 0), None, "pt"),
            (0, (1, 1, 0), 1, "dn"),
            (0, (1, 1, 0), None, "pt"),
            (0, (0, 2, 0), None, "pt"),
            (1, (0, 2, 0), None, "x"),
            (1, (0, 2, 0), None, "pt"),
            (1, (1, 3, 0), None, "pt"),
            (1, (1, 1, 0), None, "pt"),
        ],
        4: [
            (0, (1, 2, 0), None, "pt"),
            (1, (1, 2, 0), None, "pt"),
        ],
    }
    devs = {"x": x_to, "up": y_up, "dn": y_dn, "pt": partner}

    def arrived(h, iv, where):
        halves = where[1] == 2 and where[2] == 0 and not (iv and where[0] == 1)
        slot = place(*where)
        for part in ((0, 1) if halves else (None,)):
            kv_hop(h, iv, slot, part, partner, 0).wait_recv()

    first_sem = {1: 0, 2: 8, 3: 22, 4: 31}

    def stage(n, h):
        seen = set()
        for i, (iv, where, part, dev) in enumerate(SENDS[n]):
            if n > 1 and (iv, where) not in seen:
                seen.add((iv, where))
                arrived(h, iv, where)
            kv_hop(h, iv, place(*where), part, devs[dev], first_sem[n] + i).start()

    loads[2].wait()
    hid = hidden[...]
    kp = jnp.dot(hid, w3[1], preferred_element_type=F32)
    for h in range(heads):
        x = kp[:, h * HD : (h + 1) * HD]
        x = x * lax.rsqrt(jnp.mean(x * x, axis=-1, keepdims=True) + 1e-06) * k_gain[...]
        kbuf[h, s] = x.astype(BF16)
    vp = jnp.dot(hid, w3[2], preferred_element_type=F32)
    for h in range(heads):
        vbuf[h, s] = jnp.transpose(vp[:, h * HD : (h + 1) * HD]).astype(BF16)
        if h < 2:
            stage(1, h)
    qp = jnp.dot(hid, w3[0], preferred_element_type=F32)
    for h in range(heads):
        x = qp[:, h * HD : (h + 1) * HD]
        x = x * lax.rsqrt(jnp.mean(x * x, axis=-1, keepdims=True) + 1e-06) * q_gain[...]
        qbuf[h] = jnp.transpose(x).astype(BF16)
    stage(2, 0)
    stage(1, 2)
    stage(3, 0)

    w_r1.wait_recv()
    w_r2.wait_recv()
    w_p3 = w_hop(2, 0, NV, partner, 15)
    w_p3.start()

    bias = jnp.where(alive > 0.5, 0.0, -1e30)
    coef = math.log2(math.e) / math.sqrt(HD)

    def attend(h, g, carry):
        for dy in range(4):
            for iv in (0, 1):
                arrived(h, iv, (g, dy, 1))
        q = qbuf[h]

        def step(j, carry):
            m, l, acc = carry
            slot = mod(xl + g, 2) * 8 + lax.rem(y + j // 2, 4) * 2 + lax.rem(core + j, 2)
            st = jnp.dot(kbuf[h, slot], q, preferred_element_type=F32)
            st = st * coef + bias
            new = jnp.maximum(m, jnp.max(st, axis=0, keepdims=True))
            alpha = jnp.exp2(m - new)
            p = jnp.exp2(st - new)
            l = l * alpha + jnp.sum(p, axis=0, keepdims=True)
            acc = acc * alpha + jnp.dot(
                vbuf[h, slot], p.astype(BF16), preferred_element_type=F32
            )
            return new, l, acc

        return lax.fori_loop(0, 8, step, carry)

    def fresh():
        return (
            jnp.full((1, nloc), -1e30, F32),
            jnp.zeros((1, nloc), F32),
            jnp.zeros((HD, nloc), F32),
        )

    og = []
    for h in range(heads):
        og.append(
            vae_gather(
                lambda slot, lo, n, h=h: obuf.at[slot, pl.ds(lo, n), pl.ds(h * HD, HD)],
                nloc,
                lambda i, h=h: osend.at[h, i],
                lambda i, h=h: orecv.at[h, i],
            )
        )

    def finish(h, carry):
        m, l, acc = carry
        obuf[v, :, pl.ds(h * HD, HD)] = jnp.transpose(acc / l).astype(BF16)

    c = attend(0, 0, fresh())
    stage(2, 1)
    stage(4, 0)
    c = attend(0, 1, c)
    stage(3, 1)
    stage(2, 2)
    finish(0, c)
    og[0][0]()
    c = attend(1, 0, fresh())
    stage(4, 1)
    stage(3, 2)
    og[0][1]()
    c = attend(1, 1, c)
    og[0][2]()
    finish(1, c)
    og[1][0]()
    c = attend(2, 0, fresh())
    stage(4, 2)
    og[1][1]()
    c = attend(2, 1, c)
    og[1][2]()
    finish(2, c)
    og[2][0]()
    w_pt.wait_recv()
    w_p1.wait_recv()
    w_p2.wait_recv()
    w_p3.wait_recv()
    og[0][3]()
    og[1][3]()
    og[2][1]()

    def project(lo, n, start):
        def add(u, acc):
            return acc + jnp.dot(
                obuf[u, :, pl.ds(lo, n)], wcols[u, pl.ds(lo, n), :], preferred_element_type=F32
            )

        return lax.fori_loop(0, NV, add, start)

    mixed = project(0, 2 * HD, jnp.zeros((nloc, cols), F32))
    og[2][2]()
    og[2][3]()
    mixed = project(2 * HD, HD, mixed)
    here = pl.ds(pl.multiple_of(v * cols, 128), cols)
    resid = tokens[:, here].astype(F32)
    result[...] = ((resid + gate[:, here] * mixed) * alive).astype(BF16)

    for h in range(heads):
        og[h][4]()
        for n in (1, 2, 3, 4):
            for i, (iv, where, part, dev) in enumerate(SENDS[n]):
                kv_hop(h, iv, place(*where), part, devs[dev], first_sem[n] + i).wait_send()
    for c in (w_up, w_dn, w_pt, w_r1, w_p1, w_r2, w_p2, w_p3):
        c.wait_send()


def body(
    video, frame_counts, conv_weight, conv_bias, norm_gain, norm_bias, embed_weight, embed_bias,
    shift, scale, gate, qkv_weight, q_gain, k_gain, out_weight,
):
    fdev, pdev, chans = video.shape
    rows = fdev * pdev
    dwidth = embed_weight.shape[1]
    cols = qkv_weight.shape[2]
    heads = cols // HD
    nloc = NV * rows
    vm = pl.BlockSpec(memory_space=pltpu.VMEM)
    hbm = pl.BlockSpec(memory_space=pl.ANY)
    dma = pltpu.SemaphoreType.DMA
    out = pl.pallas_call(
        fused_kernel,
        name="fused",
        out_shape=jax.ShapeDtypeStruct((nloc, cols), BF16),
        in_specs=[
            vm, pl.BlockSpec(memory_space=pltpu.SMEM), hbm, vm, vm, vm, hbm, vm, vm, vm, vm, hbm,
            vm, vm, hbm,
        ],
        out_specs=vm,
        scratch_shapes=[
            pltpu.VMEM((3, chans, chans), F32),
            pltpu.VMEM((chans, dwidth), BF16),
            pltpu.VMEM((3, dwidth, cols), BF16),
            pltpu.VMEM((rows, chans), F32),
            pltpu.VMEM((3, chans, chans), BF16),
            pltpu.VMEM((3, chans, chans), BF16),
            pltpu.VMEM((NV, 2, chans), F32),
            pltpu.VMEM((NS, 2, chans), F32),
            pltpu.VMEM((NV, rows, chans), BF16),
            pltpu.VMEM((nloc, dwidth), BF16),
            pltpu.VMEM((nloc, dwidth), BF16),
            pltpu.VMEM((heads, NS, nloc, HD), BF16),
            pltpu.VMEM((heads, NS, HD, nloc), BF16),
            pltpu.VMEM((heads, HD, nloc), BF16),
            pltpu.VMEM((NV, nloc, cols), BF16),
            pltpu.VMEM((NV, cols, cols), BF16),
            dma((4,)),
            dma((2,)),
            dma((NV,)),
            dma((NV,)),
            dma((NS,)),
            dma((NS,)),
            dma((9,)),
            dma((9,)),
            dma((16,)),
            dma((16,)),
            dma((heads, 33)),
            dma((heads, NS, 2)),
            dma((heads, NS, 2)),
            dma((heads, 9)),
            dma((heads, 9)),
        ],
        compiler_params=pltpu.CompilerParams(
            collective_id=0, has_side_effects=True, vmem_limit_bytes=62 * 2**20
        ),
    )(
        video.reshape(rows, chans), frame_counts, conv_weight, conv_bias.reshape(1, -1),
        norm_gain.reshape(1, -1), norm_bias.reshape(1, -1), embed_weight,
        embed_bias.reshape(1, -1), shift.reshape(1, -1), scale.reshape(1, -1),
        gate.reshape(1, -1), jnp.transpose(qkv_weight, (1, 0, 2)), q_gain.reshape(1, -1),
        k_gain.reshape(1, -1), out_weight,
    )
    return out.reshape(fdev * NV, pdev, cols)


def solution(mesh):
    in_specs = (
        P("vae", "seq", None), P(), P(), P(), P(), P(), P(), P(), P(), P(), P(),
        P(None, None, "vae"), P(), P(), P("vae", None),
    )
    return jax.shard_map(
        body, mesh=mesh, in_specs=in_specs, out_specs=P(None, "seq", "vae"), check_vma=False
    )
```

```python
import functools
import math

import jax
import jax.numpy as jnp
from jax import lax
from jax.experimental import pallas as pl
from jax.experimental.pallas import tpu as pltpu
from jax.sharding import PartitionSpec as P

GROUPS = 32
HD = 128
NV = 8
NS = 16
F32 = jnp.float32
BF16 = jnp.bfloat16
MESH = pl.DeviceIdType.MESH
UNROLL = 4


def mod(a, n):
    return lax.rem(a + n, n)


def fused_kernel(
    video, counts, conv_w_hbm, conv_b, norm_g, norm_b, embed_w_hbm, embed_b, shift, scale,
    gate, w3_hbm, q_gain, k_gain, out_w,
    result,
    conv_w, embed_w, w3,
    halo, w_hi, w_lo, sums_v, sums_s, act, tokens, hidden,
    kbuf, vbuf, qbuf, obuf, wcols, score_a, score_b, k_tail,
    load_sem, halo_sem, ssem1, rsem1, ssem2, rsem2, asend, arecv,
    wsend, wrecv, ksend, krecv, vrecv, osend, orecv,
):
    v = lax.axis_index("vae")
    s = lax.axis_index("seq")
    rows, chans = video.shape
    pdev = 16
    width = chans // GROUPS
    dwidth = embed_b.shape[1]
    cols = dwidth // NV
    heads = cols // HD
    nloc = NV * rows

    loads = [
        pltpu.make_async_copy(conv_w_hbm, conv_w, load_sem.at[0]),
        pltpu.make_async_copy(embed_w_hbm, embed_w, load_sem.at[1]),
        pltpu.make_async_copy(w3_hbm, w3, load_sem.at[2]),
    ]
    for c in loads:
        c.start()

    xl = s // 8
    y = lax.rem(s, 8) // 2
    core = lax.rem(s, 2)
    r = lax.rem(s, 8)

    def place(dx, dy, dc):
        return mod(xl + dx, 2) * 8 + mod(y + dy, 4) * 2 + mod(core + dc, 2)

    part_rows = cols // 8
    own_w = pltpu.make_async_copy(
        out_w.at[pl.ds(r * part_rows, part_rows), pl.ds(pl.multiple_of(v * cols, 128), cols)],
        wcols.at[v, pl.ds(r * part_rows, part_rows)],
        load_sem.at[3],
    )
    own_w.start()

    barrier = pltpu.get_barrier_semaphore()
    for d in range(1, NV):
        pl.semaphore_signal(barrier, inc=1, device_id=(mod(v + d, NV), s), device_id_type=MESH)
    for d in range(1, NS):
        pl.semaphore_signal(barrier, inc=1, device_id=(v, mod(s + d, NS)), device_id_type=MESH)

    @pl.when(v == 0)
    def _():
        halo[...] = jnp.zeros_like(halo)

    pl.semaphore_wait(barrier, NV - 1 + NS - 1)
    halo_copy = pltpu.make_async_remote_copy(
        src_ref=video, dst_ref=halo, send_sem=halo_sem.at[0], recv_sem=halo_sem.at[1],
        device_id=(mod(v + 1, NV), s), device_id_type=MESH,
    )

    @pl.when(v < NV - 1)
    def _():
        halo_copy.start()

    w_first = []
    for d in range(1, NV):
        u = mod(v + d, NV)
        c = pltpu.make_async_remote_copy(
            src_ref=out_w.at[
                pl.ds(r * part_rows, part_rows), pl.ds(pl.multiple_of(u * cols, 128), cols)
            ],
            dst_ref=wcols.at[v, pl.ds(r * part_rows, part_rows)],
            send_sem=wsend.at[d], recv_sem=wrecv.at[d],
            device_id=(u, s), device_id_type=MESH,
        )
        c.start()
        w_first.append(c)

    loads[0].wait()
    for tap in range(3):
        w = conv_w[tap]
        hi = w.astype(BF16)
        w_hi[tap] = hi
        w_lo[tap] = (w - hi.astype(F32)).astype(BF16)

    mine = counts[v]
    before = counts[jnp.maximum(v - 1, 0)]

    @pl.when(v > 0)
    def _():
        halo_copy.wait_recv()

    prior = jnp.where(
        before == 2, halo[0:32], jnp.where(before == 3, halo[16:48], halo[32:64])
    )
    ext = jnp.concatenate([prior, video[...]], 0)
    e_hi = ext.astype(BF16)
    e_lo = (ext - e_hi.astype(F32)).astype(BF16)
    both = jnp.zeros((2 * rows, chans), F32)
    low = jnp.zeros((rows, chans), F32)
    for tap in range(3):
        a = 32 - 16 * tap
        x_hi = e_hi[a : a + rows]
        both += jnp.dot(
            jnp.concatenate([x_hi, e_lo[a : a + rows]], 0), w_hi[tap], preferred_element_type=F32
        )
        low += jnp.dot(x_hi, w_lo[tap], preferred_element_type=F32)
    conv = both[:rows] + (both[rows:] + low) + conv_b[...]
    row_frame = lax.broadcasted_iota(jnp.int32, (rows, chans), 0) // pdev
    masked = jnp.where(row_frame < mine, conv, 0.0)
    first = jnp.sum(masked, axis=0, keepdims=True)
    second = jnp.sum(masked * conv, axis=0, keepdims=True)
    sums_v[v] = jnp.concatenate([first, second], 0)

    @pl.when(v < NV - 1)
    def _():
        halo_copy.wait_send()

    sends = []
    for d in range(1, NV):
        c = pltpu.make_async_remote_copy(
            src_ref=sums_v.at[v], dst_ref=sums_v.at[v], send_sem=ssem1.at[d], recv_sem=rsem1.at[d],
            device_id=(mod(v + d, NV), s), device_id_type=MESH,
        )
        c.start()
        sends.append(c)
    gi = lax.broadcasted_iota(jnp.int32, (chans, chans), 0) // width
    gj = lax.broadcasted_iota(jnp.int32, (chans, chans), 1) // width
    same = jnp.where(gi == gj, 1.0, 0.0).astype(BF16)
    live = counts[0]
    for u in range(1, NV):
        live += counts[u]
    for c in sends:
        c.wait()
    total = sums_v[0]
    for u in range(1, NV):
        total += sums_v[u]
    sums_s[s] = total
    sends = []
    for d in range(1, NS):
        c = pltpu.make_async_remote_copy(
            src_ref=sums_s.at[s], dst_ref=sums_s.at[s], send_sem=ssem2.at[d], recv_sem=rsem2.at[d],
            device_id=(v, mod(s + d, NS)), device_id_type=MESH,
        )
        c.start()
        sends.append(c)

    def w_hop(dy, lo, n, dev, sem):
        rr = mod(y + dy, 4) * 2 + core
        ref = wcols.at[pl.ds(lo, n), pl.ds(rr * part_rows, part_rows)]
        return pltpu.make_async_remote_copy(
            src_ref=ref, dst_ref=ref, send_sem=wsend.at[sem], recv_sem=wrecv.at[sem],
            device_id=(v, dev), device_id_type=MESH,
        )

    partner = place(0, 0, 1)
    y_up, y_dn = place(0, 1, 0), place(0, 3, 0)
    w_up = w_hop(0, 0, NV, y_up, 8)
    w_dn = w_hop(0, 0, NV, y_dn, 9)
    w_pt = w_hop(0, 0, NV, partner, 10)

    own_w.wait()
    for c in w_first:
        c.wait()
    for c in sends:
        c.wait()
    w_up.start()
    w_dn.start()
    w_pt.start()
    total = sums_s[0]
    for u in range(1, NS):
        total += sums_s[u]
    p1 = total.astype(BF16)
    r1 = total - p1.astype(F32)
    p2 = r1.astype(BF16)
    p3 = (r1 - p2.astype(F32)).astype(BF16)
    grouped = (
        jnp.dot(p3, same, preferred_element_type=F32)
        + jnp.dot(p2, same, preferred_element_type=F32)
        + jnp.dot(p1, same, preferred_element_type=F32)
    )
    number = live.astype(F32) * (pdev * NS * width)
    mean = grouped[0:1] / number
    var = grouped[1:2] / number - mean * mean
    yv = (conv - mean) * lax.rsqrt(var + 1e-06) * norm_g[...] + norm_b[...]
    act[v] = (yv / (1.0 + jnp.exp(-yv))).astype(BF16)

    far = mod(v + 4, NV)
    base = (v // 4) * 4
    fbase = 4 - base
    z = lax.rem(v, 4)
    up, down = mod(z + 1, 4), mod(z - 1, 4)

    def vae_gather(view, n, send, recv):
        half = n // 2

        def hop(slot, lo, cnt, dev, sem):
            ref = view(slot, lo, cnt)
            return pltpu.make_async_remote_copy(
                src_ref=ref, dst_ref=ref, send_sem=send(sem), recv_sem=recv(sem),
                device_id=(dev, s), device_id_type=MESH,
            )

        far_c = hop(v, 0, n, far, 0)
        up_c = hop(v, 0, n, base + up, 1)
        dn_c = hop(v, 0, n, base + down, 2)
        fup_c = hop(far, 0, n, base + up, 3)
        fdn_c = hop(far, 0, n, base + down, 4)
        o1 = hop(base + down, 0, half, base + up, 5)
        o2 = hop(base + up, half, half, base + down, 6)
        o3 = hop(fbase + down, 0, half, base + up, 7)
        o4 = hop(fbase + up, half, half, base + down, 8)

        def one():
            far_c.start()
            up_c.start()
            dn_c.start()

        def two():
            far_c.wait_recv()
            fup_c.start()
            fdn_c.start()
            up_c.wait_recv()
            o1.start()
            dn_c.wait_recv()
            o2.start()

        def three():
            fup_c.wait_recv()
            o3.start()
            fdn_c.wait_recv()
            o4.start()

        def four():
            for c in (o1, o2, o3, o4):
                c.wait_recv()

        def five():
            for c in (far_c, up_c, dn_c, fup_c, fdn_c, o1, o2, o3, o4):
                c.wait_send()

        return one, two, three, four, five

    g = vae_gather(
        lambda slot, lo, n: act.at[slot, pl.ds(lo, n)],
        rows,
        lambda i: asend.at[i],
        lambda i: arecv.at[i],
    )
    g[0]()
    g[1]()
    g[2]()
    g[3]()
    g[4]()

    idx = lax.broadcasted_iota(jnp.int32, (nloc, 1), 0)
    limit = jnp.zeros((nloc, 1), jnp.int32)
    for u in range(NV):
        limit = jnp.where(idx // rows == u, counts[u], limit)
    alive = (lax.rem(idx, rows) // pdev < limit).astype(F32)
    loads[1].wait()
    a = act[...].reshape(nloc, chans)
    tile = 512
    acc = jnp.zeros((nloc, 128), F32)
    for t in range(dwidth // tile):
        sl = pl.ds(t * tile, tile)
        tok = jnp.dot(a, embed_w[:, sl], preferred_element_type=F32) + embed_b[:, sl]
        tok = (tok * alive).astype(BF16)
        tokens[:, sl] = tok
        tf = tok.astype(F32)
        for q in range(tile // 128):
            acc += tf[:, q * 128 : (q + 1) * 128]
    w_up.wait_recv()
    w_r1 = w_hop(3, 0, NV // 2, y_up, 11)
    w_p1 = w_hop(3, 0, NV, partner, 12)
    w_r1.start()
    w_p1.start()
    w_dn.wait_recv()
    w_r2 = w_hop(1, NV // 2, NV // 2, y_dn, 13)
    w_p2 = w_hop(1, 0, NV, partner, 14)
    w_r2.start()
    w_p2.start()
    mu = jnp.sum(acc, axis=1, keepdims=True) * (1.0 / dwidth)
    acc = jnp.zeros((nloc, 128), F32)
    for t in range(dwidth // tile):
        tf = tokens[:, pl.ds(t * tile, tile)].astype(F32) - mu
        for q in range(tile // 128):
            cut = tf[:, q * 128 : (q + 1) * 128]
            acc += cut * cut
    inv = lax.rsqrt(jnp.sum(acc, axis=1, keepdims=True) * (1.0 / dwidth) + 1e-06)
    for t in range(dwidth // tile):
        sl = pl.ds(t * tile, tile)
        tf = tokens[:, sl].astype(F32) - mu
        hidden[:, sl] = (tf * inv * (1.0 + scale[:, sl]) + shift[:, sl]).astype(BF16)

    x_to = place(1, 0, 0)

    def kv_hop(h, is_v, slot, part, dev, sem):
        buf, rec = (vbuf, vrecv) if is_v else (kbuf, krecv)
        n = HD if is_v else nloc
        if part is None:
            ref, ri = buf.at[h, slot], 0
        else:
            ref, ri = buf.at[h, slot, pl.ds(part * (n // 2), n // 2)], part
        return pltpu.make_async_remote_copy(
            src_ref=ref, dst_ref=ref, send_sem=ksend.at[h, sem], recv_sem=rec.at[h, slot, ri],
            device_id=(v, dev), device_id_type=MESH,
        )

    own = (0, 0, 0)
    X_FIRST = {
        1: [(own, None, dev) for dev in ("x", "up", "dn", "pt")],
        2: [((1, 0, 0), None, dev) for dev in ("up", "dn", "pt")]
        + [((0, 3, 0), 0, "up"), ((0, 3, 0), None, "pt")]
        + [((0, 1, 0), 1, "dn"), ((0, 1, 0), None, "pt")],
        3: [((1, 3, 0), 0, "up"), ((1, 3, 0), None, "pt")]
        + [((1, 1, 0), 1, "dn"), ((1, 1, 0), None, "pt"), ((0, 2, 0), None, "pt")],
        4: [((1, 2, 0), None, "pt")],
    }
    Y_FIRST = {
        1: X_FIRST[1],
        2: [((0, 3, 0), 0, "up"), ((0, 3, 0), None, "x"), ((0, 3, 0), None, "pt")]
        + [((0, 1, 0), 1, "dn"), ((0, 1, 0), None, "x"), ((0, 1, 0), None, "pt")]
        + [((1, 0, 0), None, "pt")],
        3: [((0, 2, 0), None, "x"), ((0, 2, 0), None, "pt")]
        + [((1, 3, 0), None, "pt"), ((1, 1, 0), None, "pt")],
        4: [((1, 2, 0), None, "pt")],
    }

    def x_first(h, iv):
        return iv == 0 or h >= 1

    def sends_of(h, n):
        return [
            (iv, *entry)
            for iv in (0, 1)
            for entry in (X_FIRST if x_first(h, iv) else Y_FIRST)[n]
        ]

    devs = {"x": x_to, "up": y_up, "dn": y_dn, "pt": partner}

    def arrived(h, iv, where):
        halves = where[1] == 2 and where[2] == 0 and (x_first(h, iv) or where[0] == 0)
        slot = place(*where)
        for part in ((0, 1) if halves else (None,)):
            kv_hop(h, iv, slot, part, partner, 0).wait_recv()

    def first_sem(h, n):
        return sum(len(sends_of(h, k)) for k in range(1, n))

    def stage(n, h, only=None):
        seen = set()
        for i, (iv, where, part, dev) in enumerate(sends_of(h, n)):
            if only is not None and iv != only:
                continue
            if n > 1 and (iv, where) not in seen:
                seen.add((iv, where))
                arrived(h, iv, where)
            kv_hop(h, iv, place(*where), part, devs[dev], first_sem(h, n) + i).start()

    loads[2].wait()
    hid = hidden[...]
    kp = jnp.dot(hid, w3[1], preferred_element_type=F32)
    for h in range(heads):
        x = kp[:, h * HD : (h + 1) * HD]
        x = x * lax.rsqrt(jnp.mean(x * x, axis=-1, keepdims=True) + 1e-06) * k_gain[...]
        kbuf[h, s] = x.astype(BF16)
        if h == 0:
            stage(1, 0, 0)
    vp = jnp.dot(hid, w3[2], preferred_element_type=F32)
    for h in range(heads):
        vbuf[h, s] = jnp.transpose(vp[:, h * HD : (h + 1) * HD]).astype(BF16)
        if h == 0:
            stage(1, 0, 1)
    qp = jnp.dot(hid, w3[0], preferred_element_type=F32)
    for h in range(heads):
        x = qp[:, h * HD : (h + 1) * HD]
        x = x * lax.rsqrt(jnp.mean(x * x, axis=-1, keepdims=True) + 1e-06) * q_gain[...]
        qbuf[h] = jnp.transpose(x).astype(BF16)
    stage(2, 0)
    stage(1, 1)
    stage(3, 0)

    w_r1.wait_recv()
    w_r2.wait_recv()
    w_p3 = w_hop(2, 0, NV, partner, 15)
    w_p3.start()

    tail_row = lax.broadcasted_iota(jnp.int32, (HD, nloc), 0)
    q_tail = jnp.where(tail_row == 0, 1.0, 0.0).astype(BF16)
    tail_col = lax.broadcasted_iota(jnp.int32, (nloc, HD), 1)
    k_tail[...] = jnp.where(tail_col == 0, jnp.where(alive > 0.5, 0.0, -1e30), 0.0).astype(BF16)
    v_tail = jnp.ones((16, nloc), BF16)
    coef = math.log2(math.e) / math.sqrt(HD)

    def attend(h, g, carry):
        for dy in range(4):
            for iv in (0, 1):
                arrived(h, iv, (g, dy, 1))
        q = jnp.concatenate([qbuf[h], q_tail], 0)

        def score(j):
            jj = lax.rem(j, 8)
            k = jnp.concatenate([kbuf[h, where(jj)], k_tail[...]], 1)
            return jnp.dot(k, q, preferred_element_type=F32)

        def where(j):
            return mod(xl + g, 2) * 8 + lax.rem(y + j // 2, 4) * 2 + lax.rem(core + j, 2)

        def soft(st, j, carry):
            m, acc = carry
            new = jnp.maximum(m, jnp.max(st, axis=0, keepdims=True))
            alpha = jnp.exp2((m - new) * coef)
            p = jnp.exp2((st - new) * coef).astype(BF16)
            vv = jnp.concatenate([vbuf[h, where(j)], v_tail], 0)
            return new, acc * alpha + jnp.dot(vv, p, preferred_element_type=F32)

        score_a[...] = score(0)

        def step(i, carry):
            for u in range(UNROLL):
                j = UNROLL * i + u
                now, later = (score_a, score_b) if u % 2 == 0 else (score_b, score_a)
                later[...] = score(j + 1)
                carry = soft(now[...], j, carry)
            return carry

        return lax.fori_loop(0, 8 // UNROLL, step, carry)

    def fresh():
        return (
            jnp.full((1, nloc), -1e30, F32),
            jnp.zeros((HD + 16, nloc), F32),
        )

    og = []
    for h in range(heads):
        og.append(
            vae_gather(
                lambda slot, lo, n, h=h: obuf.at[slot, pl.ds(lo, n), pl.ds(h * HD, HD)],
                nloc,
                lambda i, h=h: osend.at[h, i],
                lambda i, h=h: orecv.at[h, i],
            )
        )

    def finish(h, carry):
        _, acc = carry
        out = acc[:HD] / acc[HD : HD + 1]
        obuf[v, :, pl.ds(h * HD, HD)] = jnp.transpose(out).astype(BF16)

    c = attend(0, 0, fresh())
    stage(2, 1)
    stage(4, 0)
    c = attend(0, 1, c)
    finish(0, c)
    og[0][0]()
    stage(1, 2)
    stage(3, 1)
    og[0][1]()
    c = attend(1, 0, fresh())
    stage(2, 2)
    stage(4, 1)
    og[0][2]()
    c = attend(1, 1, c)
    finish(1, c)
    og[1][0]()
    stage(3, 2)
    og[1][1]()
    c = attend(2, 0, fresh())
    og[1][2]()
    stage(4, 2)
    c = attend(2, 1, c)
    finish(2, c)
    og[2][0]()
    w_pt.wait_recv()
    w_p1.wait_recv()
    w_p2.wait_recv()
    w_p3.wait_recv()
    og[2][1]()
    og[0][3]()
    og[1][3]()
    og[2][2]()

    def project(lo, n, start):
        def add(u, acc):
            return acc + jnp.dot(
                obuf[u, :, pl.ds(lo, n)], wcols[u, pl.ds(lo, n), :], preferred_element_type=F32
            )

        return lax.fori_loop(0, NV, add, start)

    mixed = project(0, 2 * HD, jnp.zeros((nloc, cols), F32))
    og[2][3]()
    mixed = project(2 * HD, HD, mixed)
    here = pl.ds(pl.multiple_of(v * cols, 128), cols)
    resid = tokens[:, here].astype(F32)
    result[...] = ((resid + gate[:, here] * mixed) * alive).astype(BF16)

    for h in range(heads):
        og[h][4]()
        for n in (1, 2, 3, 4):
            for i, (iv, where, part, dev) in enumerate(sends_of(h, n)):
                kv_hop(h, iv, place(*where), part, devs[dev], first_sem(h, n) + i).wait_send()
    for c in (w_up, w_dn, w_pt, w_r1, w_p1, w_r2, w_p2, w_p3):
        c.wait_send()


def body(
    video, frame_counts, conv_weight, conv_bias, norm_gain, norm_bias, embed_weight, embed_bias,
    shift, scale, gate, qkv_weight, q_gain, k_gain, out_weight,
):
    fdev, pdev, chans = video.shape
    rows = fdev * pdev
    dwidth = embed_weight.shape[1]
    cols = qkv_weight.shape[2]
    heads = cols // HD
    nloc = NV * rows
    vm = pl.BlockSpec(memory_space=pltpu.VMEM)
    hbm = pl.BlockSpec(memory_space=pl.ANY)
    dma = pltpu.SemaphoreType.DMA
    out = pl.pallas_call(
        fused_kernel,
        name="fused",
        out_shape=jax.ShapeDtypeStruct((nloc, cols), BF16),
        in_specs=[
            vm, pl.BlockSpec(memory_space=pltpu.SMEM), hbm, vm, vm, vm, hbm, vm, vm, vm, vm, hbm,
            vm, vm, hbm,
        ],
        out_specs=vm,
        scratch_shapes=[
            pltpu.VMEM((3, chans, chans), F32),
            pltpu.VMEM((chans, dwidth), BF16),
            pltpu.VMEM((3, dwidth, cols), BF16),
            pltpu.VMEM((rows, chans), F32),
            pltpu.VMEM((3, chans, chans), BF16),
            pltpu.VMEM((3, chans, chans), BF16),
            pltpu.VMEM((NV, 2, chans), F32),
            pltpu.VMEM((NS, 2, chans), F32),
            pltpu.VMEM((NV, rows, chans), BF16),
            pltpu.VMEM((nloc, dwidth), BF16),
            pltpu.VMEM((nloc, dwidth), BF16),
            pltpu.VMEM((heads, NS, nloc, HD), BF16),
            pltpu.VMEM((heads, NS, HD, nloc), BF16),
            pltpu.VMEM((heads, HD, nloc), BF16),
            pltpu.VMEM((NV, nloc, cols), BF16),
            pltpu.VMEM((NV, cols, cols), BF16),
            pltpu.VMEM((nloc, nloc), F32),
            pltpu.VMEM((nloc, nloc), F32),
            pltpu.VMEM((nloc, HD), BF16),
            dma((4,)),
            dma((2,)),
            dma((NV,)),
            dma((NV,)),
            dma((NS,)),
            dma((NS,)),
            dma((9,)),
            dma((9,)),
            dma((16,)),
            dma((16,)),
            dma((heads, 34)),
            dma((heads, NS, 2)),
            dma((heads, NS, 2)),
            dma((heads, 9)),
            dma((heads, 9)),
        ],
        compiler_params=pltpu.CompilerParams(
            collective_id=0, has_side_effects=True, vmem_limit_bytes=62 * 2**20
        ),
    )(
        video.reshape(rows, chans), frame_counts, conv_weight, conv_bias.reshape(1, -1),
        norm_gain.reshape(1, -1), norm_bias.reshape(1, -1), embed_weight,
        embed_bias.reshape(1, -1), shift.reshape(1, -1), scale.reshape(1, -1),
        gate.reshape(1, -1), jnp.transpose(qkv_weight, (1, 0, 2)), q_gain.reshape(1, -1),
        k_gain.reshape(1, -1), out_weight,
    )
    return out.reshape(fdev * NV, pdev, cols)


def solution(mesh):
    in_specs = (
        P("vae", "seq", None), P(), P(), P(), P(), P(), P(), P(), P(), P(), P(),
        P(None, None, "vae"), P(), P(), P("vae", None),
    )
    return jax.shard_map(
        body, mesh=mesh, in_specs=in_specs, out_specs=P(None, "seq", "vae"), check_vma=False
    )
```
